32 devices in a mesh: chan: 4 (over y, x), space: 8 (over z, core).
Axes of the slice: x: 2, y: 2, z: 4, core: 2. Of those that a mesh axis runs over, the one named last changes fastest.
Arguments:
- volume: bfloat16 [32, 16, 256, 128], P('space', None, 'chan'), may hold values from -6 to 6
- kernel: bfloat16 [27, 256, 256], P(None, 'chan'), may hold values from -0.078125 to 0.078125
- bias: float32 [256], P('chan'), may hold values from -3 to 3
- cotangent: bfloat16 [32, 16, 256, 128], P('space', None, 'chan'), may hold values from -6 to 6
Outputs:
- output: bfloat16 [32, 16, 256, 128], P('space', None, 'chan')
- input_grad: bfloat16 [32, 16, 256, 128], P('space', None, 'chan')
- weight_grad: float32 [27, 256, 256], P(None, 'chan')
The draws below stay inside these ranges and needn't reach their ends.
All inputs are finite; a program needn't handle non-finite values.
Results may differ from the reference program's by a relative error of at most 0.0049.
Values may be sent and summed in bfloat16 or wider, within the bound.
A program may use at most 128 MiB of HBM per device.

```python
import math
import jax
import jax.numpy as jnp
from jax import lax

CIN = 256
COUT = 256
TAPS = 27
NX = 32
NY = 16
NZ = 128


def block_scale(own_key, extent, shards, least, largest):
    gain, own = 1.0, jax.random.fold_in(own_key, 6)
    for dim, blocks in shards:
        draws = jnp.exp(jax.random.uniform(jax.random.fold_in(own, dim), (blocks,), jnp.float32, least / len(shards), largest / len(shards)))
        gain = gain * jnp.repeat(draws, extent[dim] // blocks).reshape([-1 if axis == dim else 1 for axis in range(len(extent))])
    return gain


def noise(stream_key, extent, width, bound, shards=(), held_as=jnp.bfloat16):
    drawn = width * jax.random.normal(stream_key, extent, jnp.float32)
    if shards:
        drawn = drawn * block_scale(stream_key, extent, shards, -0.22, 0.18)
    return jnp.clip(drawn, -bound, bound).astype(held_as)


def setup_inputs(seed: int = 0) -> dict:
    streams_of = jax.random.split(jax.random.key(seed), 5)
    return {
        "volume": noise(streams_of[0], (NX, NY, CIN, NZ), 1.0, 6.0, ((0, 8), (2, 4))),
        "kernel": noise(streams_of[1], (TAPS, COUT, CIN), (TAPS * CIN) ** -0.5, 0.078125, ((1, 4),)),
        "bias": noise(streams_of[2], (COUT,), 0.5, 3.0, ((0, 4),), jnp.float32),
        "cotangent": noise(streams_of[3], (NX, NY, COUT, NZ), 1.0, 6.0, ((0, 8), (2, 4))),
    }


def tap_list():
    return [(first, second, third) for first in range(3) for second in range(3) for third in range(3)]

def reference(volume, kernel, bias, cotangent):
    volume_last = jnp.transpose(volume, (0, 1, 3, 2))
    cotangent_last = jnp.transpose(cotangent, (0, 1, 3, 2))
    size_x, size_y, size_z, chans_in = volume_last.shape
    chans_out = kernel.shape[1]
    cells = size_x * size_y * size_z
    kernel_f = jnp.transpose(kernel.astype(jnp.float32), (0, 2, 1))
    padded = jnp.pad(volume_last.astype(jnp.float32), ((1, 1), (1, 1), (1, 1), (0, 0)))
    accum = jnp.zeros((cells, chans_out), jnp.float32)
    for index_tap, (first, second, third) in enumerate(tap_list()):
        slab = padded[first:first + size_x, second:second + size_y, third:third + size_z, :].reshape(cells, chans_in)
        accum = accum + jnp.dot(slab, kernel_f[index_tap], precision=lax.Precision.HIGHEST, preferred_element_type=jnp.float32)
    pre = accum + bias.astype(jnp.float32)
    sigmoid_pre = jax.nn.sigmoid(pre)
    output = (pre * sigmoid_pre).astype(jnp.bfloat16).reshape(size_x, size_y, size_z, chans_out)
    grad_pre = (cotangent_last.reshape(cells, chans_out).astype(jnp.float32) * sigmoid_pre * (1.0 + pre * (1.0 - sigmoid_pre))).astype(jnp.bfloat16)
    grad_f = grad_pre.astype(jnp.float32)
    parts = []
    for index_tap, (first, second, third) in enumerate(tap_list()):
        slab = padded[first:first + size_x, second:second + size_y, third:third + size_z, :].reshape(cells, chans_in)
        parts.append(jnp.dot(grad_f.T, slab, precision=lax.Precision.HIGHEST, preferred_element_type=jnp.float32))
    weight_grad = jnp.stack(parts) / math.sqrt(cells)
    grad_padded = jnp.pad(grad_f.reshape(size_x, size_y, size_z, chans_out), ((1, 1), (1, 1), (1, 1), (0, 0)))
    back = jnp.zeros((cells, chans_in), jnp.float32)
    for index_tap, (first, second, third) in enumerate(tap_list()):
        slab = grad_padded[2 - first:2 - first + size_x, 2 - second:2 - second + size_y, 2 - third:2 - third + size_z, :].reshape(cells, chans_out)
        back = back + jnp.dot(slab, kernel_f[index_tap].T, precision=lax.Precision.HIGHEST, preferred_element_type=jnp.float32)
    input_grad = back.astype(jnp.bfloat16).reshape(size_x, size_y, size_z, chans_in)
    return (jnp.transpose(output, (0, 1, 3, 2)), jnp.transpose(input_grad, (0, 1, 3, 2)), weight_grad)
```

```python
import functools
import math

import jax
import jax.numpy as jnp
from jax import lax
from jax.experimental import pallas as pl
from jax.experimental.pallas import tpu as pltpu
from jax.sharding import PartitionSpec as P

F32 = jnp.float32
BF16 = jnp.bfloat16
VMEM_LIMIT = 60 * 1024 * 1024


def shifted(rows, amount):
    size_z = rows.shape[1]
    lane = lax.broadcasted_iota(jnp.int32, rows.shape, 1)
    edge = 0 if amount == 1 else size_z - 1
    return jnp.where(lane == edge, 0.0, pltpu.roll(rows, amount % size_z, 1))


class Gather:
    def __init__(self, source, shape, planes, local_sem, send_sem, recv_sem, halo_send, halo_recv, peers, order):
        self.source, self.planes = source, planes
        self.local_sem, self.send_sem, self.recv_sem = local_sem, send_sem, recv_sem
        self.halo_send, self.halo_recv = halo_send, halo_recv
        self.size_x, self.size_y, self.part, self.size_z = shape
        self.peers = peers
        self.me = lax.axis_index("chan")
        self.slab = lax.axis_index("space")
        self.slabs = lax.axis_size("space")
        self.chans = self.part * peers
        self.has_lo, self.has_hi = self.slab > 0, self.slab < self.slabs - 1
        self.order = list(order)
        me = self.me
        if peers == 4:
            across = me // 2 * 2 + (1 - me % 2)
            along = (1 - me // 2) * 2 + me % 2
            self.owners = [me, across, along, 3 - me]
            self.near = [1, 2]
        else:
            self.owners = [(me + r) % peers for r in range(peers)]
            self.near = list(range(1, peers))

    def block(self, q, owner):
        rows = pl.ds(pl.multiple_of(q * self.chans + owner * self.part, self.part), self.part)
        return self.planes.at[rows, self.size_z : (self.size_y + 1) * self.size_z]

    def back(self, slot):
        return slot if self.peers == 4 else self.peers - slot

    def chan_copy(self, q, slot_held, toward, slot_there):
        return pltpu.make_async_remote_copy(
            src_ref=self.block(q, self.owners[slot_held]),
            dst_ref=self.block(q, self.owners[slot_held]),
            send_sem=self.send_sem.at[q, slot_there],
            recv_sem=self.recv_sem.at[q, slot_there],
            device_id=(self.me, self.slab) if toward is None else (self.owners[toward], self.slab),
            device_id_type=pl.DeviceIdType.MESH,
        )

    def arrived(self, q, slot):
        pltpu.make_async_remote_copy(
            src_ref=self.block(q, self.owners[slot]),
            dst_ref=self.block(q, self.owners[slot]),
            send_sem=self.send_sem.at[q, slot],
            recv_sem=self.recv_sem.at[q, slot],
            device_id=(self.owners[1], self.slab),
            device_id_type=pl.DeviceIdType.MESH,
        ).wait_recv()

    def halo_copy(self, slot, up):
        mine, theirs = (self.size_x, 0) if up else (1, self.size_x + 1)
        return pltpu.make_async_remote_copy(
            src_ref=self.block(mine, self.owners[slot]),
            dst_ref=self.block(theirs, self.owners[slot]),
            send_sem=self.halo_send.at[int(up), slot],
            recv_sem=self.halo_recv.at[int(up), slot],
            device_id=(self.me, self.slab + 1 if up else self.slab - 1),
            device_id_type=pl.DeviceIdType.MESH,
        )

    def halo_pass(self, q, slot):
        if q == self.size_x:

            @pl.when(self.has_hi)
            def _():
                self.halo_copy(slot, True).start()

        if q == 1:

            @pl.when(self.has_lo)
            def _():
                self.halo_copy(slot, False).start()

    def local_copy(self, q, y):
        rows = pl.ds(pl.multiple_of(q * self.chans + self.me * self.part, self.part), self.part)
        lanes = pl.ds(pl.multiple_of((y + 1) * self.size_z, self.size_z), self.size_z)
        return pltpu.make_async_copy(
            self.source.at[q - 1, y], self.planes.at[rows, lanes], self.local_sem.at[q]
        )

    def start_local(self):
        for q in self.order:

            def put(y, _, q=q):
                self.local_copy(q, y).start()
                return 0

            lax.fori_loop(0, self.size_y, put, 0)

    def wait_local(self, q):
        def done(y, _):
            self.local_copy(q, y).wait()
            return 0

        lax.fori_loop(0, self.size_y, done, 0)

    def clear(self):
        edge = jnp.zeros((self.planes.shape[0], self.size_z), BF16)
        self.planes[:, 0 : self.size_z] = edge
        self.planes[:, (self.size_y + 1) * self.size_z : (self.size_y + 2) * self.size_z] = edge
        cells = slice(self.size_z, (self.size_y + 1) * self.size_z)
        blank = jnp.zeros((self.chans, self.size_y * self.size_z), BF16)

        @pl.when(jnp.logical_not(self.has_lo))
        def _():
            self.planes[0 : self.chans, cells] = blank

        @pl.when(jnp.logical_not(self.has_hi))
        def _():
            self.planes[(self.size_x + 1) * self.chans : (self.size_x + 2) * self.chans, cells] = blank

    def send_own(self, stage):
        q = self.order[stage]
        for slot in self.near:
            self.chan_copy(q, 0, slot, self.back(slot)).start()
        self.halo_pass(q, 0)

    def relay(self, stage, q, slot):
        return self.peers == 4 and slot == (1 if stage % 2 else 2)

    def take_near(self, stage):
        q = self.order[stage]
        for slot in self.near:
            self.arrived(q, slot)
            if self.relay(stage, q, slot):
                self.chan_copy(q, slot, 3 - slot, 3).start()
            self.halo_pass(q, slot)
        if self.source is not None and stage + 2 < len(self.order):
            self.wait_local(self.order[stage + 2])
            self.send_own(stage + 2)

    def take_far(self, stage):
        q = self.order[stage]
        if self.peers == 4:
            self.arrived(q, 3)
            self.halo_pass(q, 3)

    def take_halo(self, up):
        @pl.when(self.has_lo if up else self.has_hi)
        def _():
            for slot in range(self.peers):
                mine, theirs = (self.size_x, 0) if up else (1, self.size_x + 1)
                pltpu.make_async_remote_copy(
                    src_ref=self.block(mine, self.owners[slot]),
                    dst_ref=self.block(theirs, self.owners[slot]),
                    send_sem=self.halo_send.at[int(up), slot],
                    recv_sem=self.halo_recv.at[int(up), slot],
                    device_id=(self.me, self.slab - 1 if up else self.slab + 1),
                    device_id_type=pl.DeviceIdType.MESH,
                ).wait_recv()

    def finish(self):
        for stage, q in enumerate(self.order):
            for slot in self.near:
                self.chan_copy(q, 0, slot, self.back(slot)).wait_send()
                if self.relay(stage, q, slot):
                    self.chan_copy(q, slot, 3 - slot, 3).wait_send()
        for up, there in ((True, self.has_hi), (False, self.has_lo)):

            @pl.when(there)
            def _(up=up):
                for slot in range(self.peers):
                    self.halo_copy(slot, up).wait_send()


def add_plane(planes, w_ref, acc, q, started, chans, size_y, size_z):
    size_x, rows, _ = acc.shape
    taps = [dx for dx in range(3) if 0 <= q - dx < size_x]
    first, last = taps[0], taps[-1] + 1
    count = 2

    def step(index, _):
        y = index * count
        total = None
        for dy in range(3):
            lanes = pl.ds(pl.multiple_of((y + dy) * size_z, size_z), count * size_z)
            part = jnp.dot(
                w_ref[first:last, dy].reshape((last - first) * rows, chans),
                planes[q * chans : (q + 1) * chans, lanes],
                preferred_element_type=F32,
            )
            total = part if total is None else total + part
        lanes = pl.ds(pl.multiple_of(y * size_z, size_z), count * size_z)
        for dx in taps:
            part = total[(dx - first) * rows : (dx - first + 1) * rows]
            if q - dx in started:
                acc[q - dx, :, lanes] += part
            else:
                acc[q - dx, :, lanes] = part
        return 0

    lax.fori_loop(0, size_y // count, step, 0)
    started.update(q - dx for dx in taps)


def tap_sum(acc, x, outs, lanes):
    return (
        acc[x, outs : 2 * outs, lanes]
        + shifted(acc[x, 0:outs, lanes], 1)
        + shifted(acc[x, 2 * outs : 3 * outs, lanes], -1)
    )


def tap_sum(acc, x, outs, lanes):
    return (
        acc[x, outs : 2 * outs, lanes]
        + shifted(acc[x, 0:outs, lanes], 1)
        + shifted(acc[x, 2 * outs : 3 * outs, lanes], -1)
    )


class Planes:
    def __init__(self, gather, w_ref, acc, finish_plane):
        self.gather, self.w_ref, self.acc, self.finish_plane = gather, w_ref, acc, finish_plane
        self.started, self.count = set(), {x: 3 for x in range(gather.size_x)}

    def add(self, q):
        g = self.gather
        add_plane(g.planes, self.w_ref, self.acc, q, self.started, g.chans, g.size_y, g.size_z)
        for dx in range(3):
            x = q - dx
            if x in self.count:
                self.count[x] -= 1
                if self.count[x] == 0:
                    self.finish_plane(x)


def plane_order(size_x):
    order = [1] + ([size_x] if size_x > 1 else []) + list(range(2, size_x))
    used = order[:-1] + [0, size_x + 1] + order[-1:]
    count, done = {x: 3 for x in range(size_x)}, []
    for q in used:
        for dx in range(3):
            if q - dx in count:
                count[q - dx] -= 1
                if count[q - dx] == 0:
                    done.append(q - dx + 1)
    return order, done


class Weights:
    def __init__(self, w_ref, blocks, got, turned, sems, gather):
        self.w_ref, self.blocks, self.got, self.turned = w_ref, blocks, got, turned
        self.local_sem, self.send_sem, self.recv_sem, self.pass_send, self.pass_recv = sems
        self.gather = gather
        self.peers, self.groups, self.outs, lanes = blocks.shape
        self.ins = gather.part
        self.each = lanes // self.ins
        self.half = self.groups // 2
        self.core = lax.rem(gather.slab, 2)
        self.partner = gather.slab + 1 - 2 * self.core

    def build(self):
        def step(k, _):
            taps = []
            for u in range(self.each):
                tap = jnp.minimum(k * self.each + u, 26)
                rows = pl.ds(pl.multiple_of(tap % 3 * self.outs, self.outs), self.outs)
                taps.append(self.w_ref[tap // 9, tap // 3 % 3, rows].astype(F32))
            for j in range(self.peers):
                part = [t[:, j * self.ins : (j + 1) * self.ins] for t in taps]
                self.blocks[j, k] = jnp.concatenate(part, axis=1).astype(BF16)
            return 0

        lax.fori_loop(0, self.groups, step, 0)

    def own(self):
        me = self.gather.me
        return pltpu.make_async_copy(self.blocks.at[me], self.got.at[me], self.local_sem)

    def copy(self, slot):
        g = self.gather
        rows = pl.ds(self.core * self.half, self.half)
        there = g.back(slot)
        return pltpu.make_async_remote_copy(
            src_ref=self.blocks.at[g.owners[slot], rows],
            dst_ref=self.got.at[g.me, rows],
            send_sem=self.send_sem.at[there],
            recv_sem=self.recv_sem.at[there],
            device_id=(g.owners[slot], g.slab),
            device_id_type=pl.DeviceIdType.MESH,
        )

    def arrival(self, slot, core, send_sem, recv_sem):
        g = self.gather
        rows = self.got.at[g.owners[slot], pl.ds(core * self.half, self.half)]
        return pltpu.make_async_remote_copy(
            src_ref=rows,
            dst_ref=rows,
            send_sem=send_sem.at[slot],
            recv_sem=recv_sem.at[slot],
            device_id=(g.me, self.partner),
            device_id_type=pl.DeviceIdType.MESH,
        )

    def send(self):
        self.own().start()
        for slot in range(1, self.peers):
            self.copy(slot).start()

    def hand_on(self):
        for slot in range(1, self.peers):
            self.arrival(slot, self.core, self.send_sem, self.recv_sem).wait_recv()
            self.arrival(slot, self.core, self.pass_send, self.pass_recv).start()

    def turn(self):
        self.own().wait()
        for slot in range(1, self.peers):
            self.arrival(slot, 1 - self.core, self.pass_send, self.pass_recv).wait_recv()

        def step(k, _):
            whole = jnp.concatenate([self.got[j, k] for j in range(self.peers)], axis=0)
            whole = whole.astype(F32).T.astype(BF16)
            for u in range(self.each):
                tap = 26 - (k * self.each + u)

                @pl.when(tap >= 0)
                def _():
                    at = jnp.maximum(tap, 0)
                    rows = pl.ds(pl.multiple_of(at % 3 * self.ins, self.ins), self.ins)
                    self.turned[at // 9, at // 3 % 3, rows] = whole[u * self.ins : (u + 1) * self.ins]

            return 0

        lax.fori_loop(0, self.groups, step, 0)

    def finish(self):
        for slot in range(1, self.peers):
            self.copy(slot).wait_send()
            self.arrival(slot, self.core, self.pass_send, self.pass_recv).wait_send()


class Reduce:
    def __init__(self, total, other, paired, mine, line, result, sems, slab, slabs, me):
        self.total, self.other, self.paired, self.mine = total, other, paired, mine
        self.line, self.result, self.me = line, result, me
        (
            self.pair_send,
            self.pair_recv,
            self.line_send,
            self.line_recv,
            self.cast_send,
            self.cast_recv,
            self.back_send,
            self.back_recv,
        ) = sems
        self.members, self.chunk, self.cols = line.shape
        self.half = self.members * self.chunk
        self.core, self.place = lax.rem(slab, 2), slab // 2
        self.partner = slab + 1 - 2 * self.core

    def rows(self, start):
        return pl.ds(pl.multiple_of(start * self.chunk, self.chunk), self.chunk)

    def member(self, r):
        return lax.rem(self.place + r, self.members)

    def remote(self, src, dst, send, recv, slab):
        return pltpu.make_async_remote_copy(
            src_ref=src,
            dst_ref=dst,
            send_sem=send,
            recv_sem=recv,
            device_id=(self.me, slab),
            device_id_type=pl.DeviceIdType.MESH,
        )

    def pair(self):
        return self.remote(self.other, self.paired, self.pair_send, self.pair_recv, self.partner)

    def along(self, r):
        return self.remote(
            self.mine.at[self.rows(self.member(r))],
            self.line.at[r],
            self.line_send.at[r],
            self.line_recv.at[r],
            self.member(r) * 2 + self.core,
        )

    def block(self, core, place):
        return self.result.at[self.rows(core * self.members + place)]

    def cast(self, r):
        own = self.block(self.core, self.place)
        slab = self.member(r) * 2 + self.core
        return self.remote(own, own, self.cast_send.at[r], self.cast_recv.at[r], slab)

    def came(self, r):
        block = self.block(self.core, self.member(self.members - r))
        return self.remote(block, block, self.cast_send.at[r], self.cast_recv.at[r], self.partner)

    def hand_back(self, r, core):
        block = self.block(core, self.member(self.members - r))
        return self.remote(block, block, self.back_send.at[r], self.back_recv.at[r], self.partner)

    def start(self):
        def step(k, _):
            rows = self.rows((1 - self.core) * self.members + k)
            self.other[self.rows(k)] = self.total[rows].astype(BF16)
            return 0

        lax.fori_loop(0, self.members, step, 0)
        self.pair().start()

    def second(self):
        self.pair().wait_recv()

        def step(k, _):
            rows = self.rows(self.core * self.members + k)
            both = self.total[rows] + self.paired[self.rows(k)].astype(F32)
            self.total[rows] = both
            self.mine[self.rows(k)] = both.astype(BF16)
            return 0

        lax.fori_loop(0, self.members, step, 0)
        for r in range(1, self.members):
            self.along(r).start()

    def third(self, scale):
        for r in range(1, self.members):
            self.along(r).wait_recv()
        rows = self.rows(self.core * self.members + self.place)
        whole = self.total[rows]
        for r in range(1, self.members):
            whole = whole + self.line[r].astype(F32)
        self.result[rows] = (whole * scale).astype(BF16)
        for r in range(1, self.members):
            self.cast(r).start()
        self.hand_back(0, self.core).start()

    def fourth(self):
        for r in range(1, self.members):
            self.came(r).wait_recv()
            self.hand_back(r, self.core).start()

    def last(self):
        for r in range(self.members):
            self.hand_back(r, 1 - self.core).wait_recv()

    def finish(self):
        self.pair().wait_send()
        for r in range(self.members):
            if r:
                self.along(r).wait_send()
                self.cast(r).wait_send()
            self.hand_back(r, self.core).wait_send()


def fused_kernel(
    peers, slabs, vol_ref, w_ref, bias_ref, cot_ref, out_ref, input_ref, weight_ref,
    planes, grads, acc, three, total, other, paired, mine, line, result, blocks, got, turned, local_sem, *sems
):
    size_x, size_y, outs, size_z = cot_ref.shape
    order, done = plane_order(size_x)
    vol = Gather(vol_ref, cot_ref.shape, planes, local_sem, *sems[0:4], peers, order)
    grad = Gather(None, cot_ref.shape, grads, None, *sems[4:8], peers, done)
    weights = Weights(w_ref, blocks, got, turned, sems[8:13], vol)
    reduce = Reduce(total, other, paired, mine, line, result, sems[13:21], vol.slab, slabs, vol.me)
    chans, cells = vol.chans, size_y * size_z

    vol.start_local()
    barrier = pltpu.get_barrier_semaphore()
    for slot in range(1, peers):
        device = (vol.owners[slot], vol.slab)
        pl.semaphore_signal(barrier, inc=1, device_id=device, device_id_type=pl.DeviceIdType.MESH)
    for r in range(1, slabs):
        device = (vol.me, lax.rem(vol.slab + r, slabs))
        pl.semaphore_signal(barrier, inc=1, device_id=device, device_id_type=pl.DeviceIdType.MESH)
    vol.clear()
    pl.semaphore_wait(barrier, peers - 1 + slabs - 1)
    for stage in range(min(2, size_x)):
        vol.wait_local(order[stage])
        vol.send_own(stage)
    grad.clear()
    total[...] = jnp.zeros_like(total)
    weights.build()
    bias = jnp.broadcast_to(bias_ref[...], (size_z, outs)).T
    mine_rows = pl.multiple_of(vol.me * outs, outs)

    def finish_forward(x):
        rows = pl.ds(pl.multiple_of((x + 1) * chans + mine_rows, outs), outs)

        def step(y, _):
            lanes = pl.ds(pl.multiple_of(y * size_z, size_z), size_z)
            pre = tap_sum(acc, x, outs, lanes) + bias
            sig = jax.nn.sigmoid(pre)
            out_ref[x, y] = (pre * sig).astype(BF16)
            held = (cot_ref[x, y].astype(F32) * sig * (1.0 + pre * (1.0 - sig))).astype(BF16)
            grads[rows, pl.ds(pl.multiple_of((y + 1) * size_z, size_z), size_z)] = held
            value = held.astype(F32)
            three[x, 0:outs, lanes] = shifted(value, -1).astype(BF16)
            three[x, outs : 2 * outs, lanes] = held
            three[x, 2 * outs : 3 * outs, lanes] = shifted(value, 1).astype(BF16)
            return 0

        lax.fori_loop(0, size_y, step, 0)
        grad.send_own(done.index(x + 1))

    def finish_input(x):
        def step(y, _):
            lanes = pl.ds(pl.multiple_of(y * size_z, size_z), size_z)
            input_ref[x, y] = tap_sum(acc, x, outs, lanes).astype(BF16)
            return 0

        lax.fori_loop(0, size_y, step, 0)

    forward = Planes(vol, w_ref, acc, finish_forward)
    stages = size_x
    for stage in range(stages):
        vol.take_near(stage)
        if stage == min(1, stages - 1):
            weights.send()
        if stage:
            vol.take_far(stage - 1)
            forward.add(order[stage - 1])
    vol.take_halo(True)
    forward.add(0)
    vol.take_halo(False)
    forward.add(size_x + 1)
    vol.take_far(stages - 1)
    forward.add(order[-1])
    weights.hand_on()

    def weight_grad(first, last):
        def step(x, _):
            for dy in range(3):
                cube = planes[pl.ds(pl.multiple_of(x * chans, chans), 3 * chans), dy * size_z : dy * size_z + cells]
                part = lax.dot_general(three[x], cube, (((1,), (1,)), ((), ())), preferred_element_type=F32)
                for dx in range(3):
                    at = (dx * 3 + dy) * 3 * outs
                    total[at : at + 3 * outs] += part[:, dx * chans : (dx + 1) * chans]
            return 0

        lax.fori_loop(first, last, step, 0)

    backward = Planes(grad, turned, acc, finish_input)
    grad.take_near(0)
    weight_grad(0, size_x // 2)
    if stages > 1:
        grad.take_near(1)
    weight_grad(size_x // 2, size_x)
    reduce.start()
    weights.turn()
    grad.take_far(0)
    later = [reduce.second, functools.partial(reduce.third, 1.0 / math.sqrt(size_x * cells * slabs)), reduce.fourth]
    for stage in range(2, stages + 1):
        backward.add(done[stage - 2])
        if later:
            later.pop(0)()
        if stage < stages:
            grad.take_near(stage)
        grad.take_far(stage - 1)
    grad.take_halo(True)
    backward.add(0)
    if later:
        later.pop(0)()
    grad.take_halo(False)
    backward.add(size_x + 1)
    while later:
        later.pop(0)()
    backward.add(done[-1])
    reduce.last()
    weight_ref[...] = result[0 : weight_ref.shape[0]].astype(F32)
    vol.finish()
    grad.finish()
    weights.finish()
    reduce.finish()


def on_device(volume, kernel, bias, cotangent):
    size_x, size_y, part, size_z = volume.shape
    taps, outs, chans = kernel.shape
    shape = jax.ShapeDtypeStruct
    flops = 2 * size_x * size_y * size_z * taps * outs * chans
    peers, slabs = lax.axis_size("chan"), lax.axis_size("space")
    each = max(1, size_z // part)
    groups = 2 * -(-taps // (2 * each))
    members = slabs // 2
    chunk = 16 * -(-taps * outs // (slabs * 16))
    whole = pl.BlockSpec(memory_space=pltpu.VMEM)
    args = (volume, kernel.reshape(3, 3, 3 * outs, chans), bias.reshape(1, outs), cotangent)
    planes = size_x + 2
    dma = pltpu.SemaphoreType.DMA
    sides = [dma((planes, peers)), dma((planes, peers)), dma((2, peers)), dma((2, peers))]
    output, input_grad, weight_grad = pl.pallas_call(
        functools.partial(fused_kernel, peers, slabs),
        out_shape=(
            shape(cotangent.shape, BF16),
            shape(volume.shape, BF16),
            shape((taps * outs, chans), F32),
        ),
        in_specs=[pl.BlockSpec(memory_space=pl.ANY)] + [whole] * 3,
        out_specs=(whole, whole, whole),
        scratch_shapes=[
            pltpu.VMEM((planes * chans, (size_y + 2) * size_z), BF16),
            pltpu.VMEM((planes * chans, (size_y + 2) * size_z), BF16),
            pltpu.VMEM((size_x, 3 * outs, size_y * size_z), F32),
            pltpu.VMEM((size_x, 3 * outs, size_y * size_z), BF16),
            pltpu.VMEM((slabs * chunk, chans), F32),
            pltpu.VMEM((members * chunk, chans), BF16),
            pltpu.VMEM((members * chunk, chans), BF16),
            pltpu.VMEM((members * chunk, chans), BF16),
            pltpu.VMEM((members, chunk, chans), BF16),
            pltpu.VMEM((slabs * chunk, chans), BF16),
            pltpu.VMEM((peers, groups, outs, each * part), BF16),
            pltpu.VMEM((peers, groups, outs, each * part), BF16),
            pltpu.VMEM((3, 3, 3 * part, chans), BF16),
            dma((planes,)),
            *sides,
            *sides,
            dma(()),
            dma((peers,)),
            dma((peers,)),
            dma((peers,)),
            dma((peers,)),
            dma(()),
            dma(()),
            *[dma((members,)) for _ in range(6)],
        ],
        compiler_params=pltpu.CompilerParams(vmem_limit_bytes=VMEM_LIMIT, collective_id=0, has_side_effects=True),
        cost_estimate=pl.CostEstimate(flops=3 * flops, bytes_accessed=8 * volume.size, transcendentals=0),
    )(*args)
    return output, input_grad, weight_grad.reshape(taps, outs, chans)


def solution(mesh):
    return jax.shard_map(
        on_device,
        mesh=mesh,
        in_specs=(
            P("space", None, "chan", None),
            P(None, "chan", None),
            P("chan"),
            P("space", None, "chan", None),
        ),
        out_specs=(
            P("space", None, "chan", None),
            P("space", None, "chan", None),
            P(None, "chan", None),
        ),
        check_vma=False,
    )
```

```python
import functools
import math

import jax
import jax.numpy as jnp
from jax import lax
from jax.experimental import pallas as pl
from jax.experimental.pallas import tpu as pltpu
from jax.sharding import PartitionSpec as P

F32 = jnp.float32
BF16 = jnp.bfloat16
VMEM_LIMIT = 60 * 1024 * 1024


def shifted(rows, amount):
    size_z = rows.shape[1]
    lane = lax.broadcasted_iota(jnp.int32, rows.shape, 1)
    edge = 0 if amount == 1 else size_z - 1
    return jnp.where(lane == edge, 0.0, pltpu.roll(rows, amount % size_z, 1))


class Gather:
    def __init__(self, source, shape, planes, local_sem, send_sem, recv_sem, halo_send, halo_recv, peers, order):
        self.source, self.planes = source, planes
        self.local_sem, self.send_sem, self.recv_sem = local_sem, send_sem, recv_sem
        self.halo_send, self.halo_recv = halo_send, halo_recv
        self.size_x, self.size_y, self.part, self.size_z = shape
        self.peers = peers
        self.me = lax.axis_index("chan")
        self.slab = lax.axis_index("space")
        self.slabs = lax.axis_size("space")
        self.chans = self.part * peers
        self.has_lo, self.has_hi = self.slab > 0, self.slab < self.slabs - 1
        self.order = list(order)
        me = self.me
        if peers == 4:
            across = me // 2 * 2 + (1 - me % 2)
            along = (1 - me // 2) * 2 + me % 2
            self.owners = [me, across, along, 3 - me]
            self.near = [1, 2]
        else:
            self.owners = [(me + r) % peers for r in range(peers)]
            self.near = list(range(1, peers))

    def block(self, q, owner, half=None):
        rows = pl.ds(pl.multiple_of(q * self.chans + owner * self.part, self.part), self.part)
        first, last = (0, 2) if half is None else (half, half + 1)
        each = self.size_y * self.size_z // 2
        return self.planes.at[rows, self.size_z + first * each : self.size_z + last * each]

    def back(self, slot):
        return slot if self.peers == 4 else self.peers - slot

    def chan_copy(self, q, slot_held, toward, slot_there, half):
        block = self.block(q, self.owners[slot_held], half)
        return pltpu.make_async_remote_copy(
            src_ref=block,
            dst_ref=block,
            send_sem=self.send_sem.at[q, slot_there, half],
            recv_sem=self.recv_sem.at[q, slot_there, half],
            device_id=(self.owners[toward], self.slab),
            device_id_type=pl.DeviceIdType.MESH,
        )

    def arrived(self, q, slot, half):
        block = self.block(q, self.owners[slot], half)
        pltpu.make_async_remote_copy(
            src_ref=block,
            dst_ref=block,
            send_sem=self.send_sem.at[q, slot, half],
            recv_sem=self.recv_sem.at[q, slot, half],
            device_id=(self.owners[1], self.slab),
            device_id_type=pl.DeviceIdType.MESH,
        ).wait_recv()

    def halo_copy(self, slot, up):
        mine, theirs = (self.size_x, 0) if up else (1, self.size_x + 1)
        return pltpu.make_async_remote_copy(
            src_ref=self.block(mine, self.owners[slot]),
            dst_ref=self.block(theirs, self.owners[slot]),
            send_sem=self.halo_send.at[int(up), slot],
            recv_sem=self.halo_recv.at[int(up), slot],
            device_id=(self.me, self.slab + 1 if up else self.slab - 1),
            device_id_type=pl.DeviceIdType.MESH,
        )

    def halo_pass(self, q, slot):
        if q == self.size_x:

            @pl.when(self.has_hi)
            def _():
                self.halo_copy(slot, True).start()

        if q == 1:

            @pl.when(self.has_lo)
            def _():
                self.halo_copy(slot, False).start()

    def local_copy(self, q, y):
        rows = pl.ds(pl.multiple_of(q * self.chans + self.me * self.part, self.part), self.part)
        lanes = pl.ds(pl.multiple_of((y + 1) * self.size_z, self.size_z), self.size_z)
        return pltpu.make_async_copy(
            self.source.at[q - 1, y], self.planes.at[rows, lanes], self.local_sem.at[q]
        )

    def start_local(self):
        for q in self.order:

            def put(y, _, q=q):
                self.local_copy(q, y).start()
                return 0

            lax.fori_loop(0, self.size_y, put, 0)

    def wait_local(self, q):
        def done(y, _):
            self.local_copy(q, y).wait()
            return 0

        lax.fori_loop(0, self.size_y, done, 0)

    def clear(self):
        edge = jnp.zeros((self.planes.shape[0], self.size_z), BF16)
        self.planes[:, 0 : self.size_z] = edge
        self.planes[:, (self.size_y + 1) * self.size_z : (self.size_y + 2) * self.size_z] = edge
        cells = slice(self.size_z, (self.size_y + 1) * self.size_z)
        blank = jnp.zeros((self.chans, self.size_y * self.size_z), BF16)

        @pl.when(jnp.logical_not(self.has_lo))
        def _():
            self.planes[0 : self.chans, cells] = blank

        @pl.when(jnp.logical_not(self.has_hi))
        def _():
            self.planes[(self.size_x + 1) * self.chans : (self.size_x + 2) * self.chans, cells] = blank

    def send_own(self, stage):
        q = self.order[stage]
        for half in range(2):
            for slot in self.near:
                self.chan_copy(q, 0, slot, self.back(slot), half).start()
        self.halo_pass(q, 0)

    def relay(self, slot, half):
        return self.peers == 4 and slot == half + 1

    def take_near(self, stage):
        q = self.order[stage]
        for half in range(2):
            for slot in self.near:
                self.arrived(q, slot, half)
                if self.relay(slot, half):
                    self.chan_copy(q, slot, 3 - slot, 3, half).start()
        for slot in self.near:
            self.halo_pass(q, slot)
        if self.source is not None and stage + 2 < len(self.order):
            self.wait_local(self.order[stage + 2])
            self.send_own(stage + 2)

    def take_far(self, stage):
        q = self.order[stage]
        if self.peers == 4:
            for half in range(2):
                self.arrived(q, 3, half)
            self.halo_pass(q, 3)

    def take_halo(self, up):
        @pl.when(self.has_lo if up else self.has_hi)
        def _():
            for slot in range(self.peers):
                mine, theirs = (self.size_x, 0) if up else (1, self.size_x + 1)
                pltpu.make_async_remote_copy(
                    src_ref=self.block(mine, self.owners[slot]),
                    dst_ref=self.block(theirs, self.owners[slot]),
                    send_sem=self.halo_send.at[int(up), slot],
                    recv_sem=self.halo_recv.at[int(up), slot],
                    device_id=(self.me, self.slab - 1 if up else self.slab + 1),
                    device_id_type=pl.DeviceIdType.MESH,
                ).wait_recv()

    def finish(self):
        for q in self.order:
            for half in range(2):
                for slot in self.near:
                    self.chan_copy(q, 0, slot, self.back(slot), half).wait_send()
                    if self.relay(slot, half):
                        self.chan_copy(q, slot, 3 - slot, 3, half).wait_send()
        for up, there in ((True, self.has_hi), (False, self.has_lo)):

            @pl.when(there)
            def _(up=up):
                for slot in range(self.peers):
                    self.halo_copy(slot, up).wait_send()


def add_plane(planes, w_ref, acc, q, started, chans, size_y, size_z):
    size_x, rows, _ = acc.shape
    taps = [dx for dx in range(3) if 0 <= q - dx < size_x]
    first, last = taps[0], taps[-1] + 1
    count = 4 if size_y % 4 == 0 else 1

    def step(index, _):
        y = index * count
        total = None
        for dy in range(3):
            lanes = pl.ds(pl.multiple_of((y + dy) * size_z, size_z), count * size_z)
            part = jnp.dot(
                w_ref[first:last, dy].reshape((last - first) * rows, chans),
                planes[q * chans : (q + 1) * chans, lanes],
                preferred_element_type=F32,
            )
            total = part if total is None else total + part
        lanes = pl.ds(pl.multiple_of(y * size_z, size_z), count * size_z)
        for dx in taps:
            part = total[(dx - first) * rows : (dx - first + 1) * rows]
            if q - dx in started:
                acc[q - dx, :, lanes] += part
            else:
                acc[q - dx, :, lanes] = part
        return 0

    lax.fori_loop(0, size_y // count, step, 0)
    started.update(q - dx for dx in taps)


def tap_sum(acc, x, outs, lanes):
    return (
        acc[x, outs : 2 * outs, lanes]
        + shifted(acc[x, 0:outs, lanes], 1)
        + shifted(acc[x, 2 * outs : 3 * outs, lanes], -1)
    )


def tap_sum(acc, x, outs, lanes):
    return (
        acc[x, outs : 2 * outs, lanes]
        + shifted(acc[x, 0:outs, lanes], 1)
        + shifted(acc[x, 2 * outs : 3 * outs, lanes], -1)
    )


class Planes:
    def __init__(self, gather, w_ref, acc, finish_plane):
        self.gather, self.w_ref, self.acc, self.finish_plane = gather, w_ref, acc, finish_plane
        self.started, self.count = set(), {x: 3 for x in range(gather.size_x)}

    def add(self, q):
        g = self.gather
        add_plane(g.planes, self.w_ref, self.acc, q, self.started, g.chans, g.size_y, g.size_z)
        for dx in range(3):
            x = q - dx
            if x in self.count:
                self.count[x] -= 1
                if self.count[x] == 0:
                    self.finish_plane(x)


def plane_order(size_x):
    order = [1] + ([size_x] if size_x > 1 else []) + list(range(2, size_x))
    used = order[:-1] + [0, size_x + 1] + order[-1:]
    count, done = {x: 3 for x in range(size_x)}, []
    for q in used:
        for dx in range(3):
            if q - dx in count:
                count[q - dx] -= 1
                if count[q - dx] == 0:
                    done.append(q - dx + 1)
    return order, done


class Weights:
    def __init__(self, w_ref, blocks, got, turned, sems, gather):
        self.w_ref, self.blocks, self.got, self.turned = w_ref, blocks, got, turned
        self.local_sem, self.send_sem, self.recv_sem, self.pass_send, self.pass_recv = sems
        self.gather = gather
        self.peers, self.groups, self.outs, lanes = blocks.shape
        self.ins = gather.part
        self.each = lanes // self.ins
        self.half = self.groups // 2
        self.core = lax.rem(gather.slab, 2)
        self.partner = gather.slab + 1 - 2 * self.core

    def build(self):
        def step(k, _):
            taps = []
            for u in range(self.each):
                tap = jnp.minimum(k * self.each + u, 26)
                rows = pl.ds(pl.multiple_of(tap % 3 * self.outs, self.outs), self.outs)
                taps.append(self.w_ref[tap // 9, tap // 3 % 3, rows].astype(F32))
            for j in range(self.peers):
                part = [t[:, j * self.ins : (j + 1) * self.ins] for t in taps]
                self.blocks[j, k] = jnp.concatenate(part, axis=1).astype(BF16)
            return 0

        lax.fori_loop(0, self.groups, step, 0)

    def own(self):
        me = self.gather.me
        return pltpu.make_async_copy(self.blocks.at[me], self.got.at[me], self.local_sem)

    def copy(self, slot):
        g = self.gather
        rows = pl.ds(self.core * self.half, self.half)
        there = g.back(slot)
        return pltpu.make_async_remote_copy(
            src_ref=self.blocks.at[g.owners[slot], rows],
            dst_ref=self.got.at[g.me, rows],
            send_sem=self.send_sem.at[there],
            recv_sem=self.recv_sem.at[there],
            device_id=(g.owners[slot], g.slab),
            device_id_type=pl.DeviceIdType.MESH,
        )

    def arrival(self, slot, core, send_sem, recv_sem):
        g = self.gather
        rows = self.got.at[g.owners[slot], pl.ds(core * self.half, self.half)]
        return pltpu.make_async_remote_copy(
            src_ref=rows,
            dst_ref=rows,
            send_sem=send_sem.at[slot],
            recv_sem=recv_sem.at[slot],
            device_id=(g.me, self.partner),
            device_id_type=pl.DeviceIdType.MESH,
        )

    def send(self):
        self.own().start()
        for slot in range(1, self.peers):
            self.copy(slot).start()

    def hand_on(self):
        for slot in range(1, self.peers):
            self.arrival(slot, self.core, self.send_sem, self.recv_sem).wait_recv()
            self.arrival(slot, self.core, self.pass_send, self.pass_recv).start()

    def turn(self):
        self.own().wait()
        for slot in range(1, self.peers):
            self.arrival(slot, 1 - self.core, self.pass_send, self.pass_recv).wait_recv()

        def step(k, _):
            whole = jnp.concatenate([self.got[j, k] for j in range(self.peers)], axis=0)
            whole = whole.astype(F32).T.astype(BF16)
            for u in range(self.each):
                tap = 26 - (k * self.each + u)

                @pl.when(tap >= 0)
                def _():
                    at = jnp.maximum(tap, 0)
                    rows = pl.ds(pl.multiple_of(at % 3 * self.ins, self.ins), self.ins)
                    self.turned[at // 9, at // 3 % 3, rows] = whole[u * self.ins : (u + 1) * self.ins]

            return 0

        lax.fori_loop(0, self.groups, step, 0)

    def finish(self):
        for slot in range(1, self.peers):
            self.copy(slot).wait_send()
            self.arrival(slot, self.core, self.pass_send, self.pass_recv).wait_send()


class Reduce:
    def __init__(self, total, other, paired, mine, line, result, sems, slab, slabs, me):
        self.total, self.other, self.paired, self.mine = total, other, paired, mine
        self.line, self.result, self.me = line, result, me
        (
            self.pair_send,
            self.pair_recv,
            self.line_send,
            self.line_recv,
            self.cast_send,
            self.cast_recv,
            self.back_send,
            self.back_recv,
        ) = sems
        self.members, self.chunk, self.cols = line.shape
        self.half = self.members * self.chunk
        self.core, self.place = lax.rem(slab, 2), slab // 2
        self.partner = slab + 1 - 2 * self.core

    def rows(self, start):
        return pl.ds(pl.multiple_of(start * self.chunk, self.chunk), self.chunk)

    def member(self, r):
        return lax.rem(self.place + r, self.members)

    def remote(self, src, dst, send, recv, slab):
        return pltpu.make_async_remote_copy(
            src_ref=src,
            dst_ref=dst,
            send_sem=send,
            recv_sem=recv,
            device_id=(self.me, slab),
            device_id_type=pl.DeviceIdType.MESH,
        )

    def pair(self):
        return self.remote(self.other, self.paired, self.pair_send, self.pair_recv, self.partner)

    def along(self, r):
        return self.remote(
            self.mine.at[self.rows(self.member(r))],
            self.line.at[r],
            self.line_send.at[r],
            self.line_recv.at[r],
            self.member(r) * 2 + self.core,
        )

    def block(self, core, place):
        return self.result.at[self.rows(core * self.members + place)]

    def cast(self, r):
        own = self.block(self.core, self.place)
        slab = self.member(r) * 2 + self.core
        return self.remote(own, own, self.cast_send.at[r], self.cast_recv.at[r], slab)

    def came(self, r):
        block = self.block(self.core, self.member(self.members - r))
        return self.remote(block, block, self.cast_send.at[r], self.cast_recv.at[r], self.partner)

    def hand_back(self, r, core):
        block = self.block(core, self.member(self.members - r))
        return self.remote(block, block, self.back_send.at[r], self.back_recv.at[r], self.partner)

    def start(self):
        def step(k, _):
            rows = self.rows((1 - self.core) * self.members + k)
            self.other[self.rows(k)] = self.total[rows].astype(BF16)
            return 0

        lax.fori_loop(0, self.members, step, 0)
        self.pair().start()

    def second(self):
        self.pair().wait_recv()

        def step(k, _):
            rows = self.rows(self.core * self.members + k)
            both = self.total[rows] + self.paired[self.rows(k)].astype(F32)
            self.total[rows] = both
            self.mine[self.rows(k)] = both.astype(BF16)
            return 0

        lax.fori_loop(0, self.members, step, 0)
        for r in range(1, self.members):
            self.along(r).start()

    def third(self, scale):
        for r in range(1, self.members):
            self.along(r).wait_recv()
        rows = self.rows(self.core * self.members + self.place)
        whole = self.total[rows]
        for r in range(1, self.members):
            whole = whole + self.line[r].astype(F32)
        self.result[rows] = (whole * scale).astype(BF16)
        for r in range(1, self.members):
            self.cast(r).start()
        self.hand_back(0, self.core).start()

    def fourth(self):
        for r in range(1, self.members):
            self.came(r).wait_recv()
            self.hand_back(r, self.core).start()

    def last(self):
        for r in range(self.members):
            self.hand_back(r, 1 - self.core).wait_recv()

    def finish(self):
        self.pair().wait_send()
        for r in range(self.members):
            if r:
                self.along(r).wait_send()
                self.cast(r).wait_send()
            self.hand_back(r, self.core).wait_send()


def fused_kernel(
    peers, slabs, vol_ref, w_ref, bias_ref, cot_ref, out_ref, input_ref, weight_ref,
    planes, grads, acc, three, total, other, paired, mine, line, result, blocks, got, turned, local_sem, *sems
):
    size_x, size_y, outs, size_z = cot_ref.shape
    order, done = plane_order(size_x)
    vol = Gather(vol_ref, cot_ref.shape, planes, local_sem, *sems[0:4], peers, order)
    grad = Gather(None, cot_ref.shape, grads, None, *sems[4:8], peers, done)
    weights = Weights(w_ref, blocks, got, turned, sems[8:13], vol)
    reduce = Reduce(total, other, paired, mine, line, result, sems[13:21], vol.slab, slabs, vol.me)
    chans, cells = vol.chans, size_y * size_z

    vol.start_local()
    barrier = pltpu.get_barrier_semaphore()
    for slot in range(1, peers):
        device = (vol.owners[slot], vol.slab)
        pl.semaphore_signal(barrier, inc=1, device_id=device, device_id_type=pl.DeviceIdType.MESH)
    for r in range(1, slabs):
        device = (vol.me, lax.rem(vol.slab + r, slabs))
        pl.semaphore_signal(barrier, inc=1, device_id=device, device_id_type=pl.DeviceIdType.MESH)
    vol.clear()
    pl.semaphore_wait(barrier, peers - 1 + slabs - 1)
    for stage in range(min(2, size_x)):
        vol.wait_local(order[stage])
        vol.send_own(stage)
    grad.clear()
    total[...] = jnp.zeros_like(total)
    weights.build()
    bias = jnp.broadcast_to(bias_ref[...], (size_z, outs)).T
    mine_rows = pl.multiple_of(vol.me * outs, outs)

    def finish_forward(x):
        rows = pl.ds(pl.multiple_of((x + 1) * chans + mine_rows, outs), outs)

        def step(y, _):
            lanes = pl.ds(pl.multiple_of(y * size_z, size_z), size_z)
            pre = tap_sum(acc, x, outs, lanes) + bias
            sig = jax.nn.sigmoid(pre)
            out_ref[x, y] = (pre * sig).astype(BF16)
            held = (cot_ref[x, y].astype(F32) * sig * (1.0 + pre * (1.0 - sig))).astype(BF16)
            grads[rows, pl.ds(pl.multiple_of((y + 1) * size_z, size_z), size_z)] = held
            value = held.astype(F32)
            three[x, 0:outs, lanes] = shifted(value, -1).astype(BF16)
            three[x, outs : 2 * outs, lanes] = held
            three[x, 2 * outs : 3 * outs, lanes] = shifted(value, 1).astype(BF16)
            return 0

        lax.fori_loop(0, size_y, step, 0)
        grad.send_own(done.index(x + 1))

    def finish_input(x):
        def step(y, _):
            lanes = pl.ds(pl.multiple_of(y * size_z, size_z), size_z)
            input_ref[x, y] = tap_sum(acc, x, outs, lanes).astype(BF16)
            return 0

        lax.fori_loop(0, size_y, step, 0)

    forward = Planes(vol, w_ref, acc, finish_forward)
    stages = size_x
    for stage in range(stages):
        vol.take_near(stage)
        if stage == min(1, stages - 1):
            weights.send()
        if stage:
            vol.take_far(stage - 1)
            forward.add(order[stage - 1])
    vol.take_halo(True)
    forward.add(0)
    vol.take_halo(False)
    forward.add(size_x + 1)
    weights.hand_on()
    vol.take_far(stages - 1)
    forward.add(order[-1])

    def weight_grad(first, last):
        def step(x, _):
            for dy in range(3):
                cube = planes[pl.ds(pl.multiple_of(x * chans, chans), 3 * chans), dy * size_z : dy * size_z + cells]
                part = lax.dot_general(three[x], cube, (((1,), (1,)), ((), ())), preferred_element_type=F32)
                for dx in range(3):
                    at = (dx * 3 + dy) * 3 * outs
                    total[at : at + 3 * outs] += part[:, dx * chans : (dx + 1) * chans]
            return 0

        lax.fori_loop(first, last, step, 0)

    backward = Planes(grad, turned, acc, finish_input)
    grad.take_near(0)
    weight_grad(0, size_x // 2)
    if stages > 1:
        grad.take_near(1)
    weight_grad(size_x // 2, size_x)
    reduce.start()
    weights.turn()
    grad.take_far(0)
    scale = 1.0 / math.sqrt(size_x * cells * slabs)
    later = [reduce.second, functools.partial(reduce.third, scale), reduce.fourth]
    for stage in range(2, stages + 1):
        backward.add(done[stage - 2])
        if stage < stages:
            grad.take_near(stage)
            if len(later) > 1:
                later.pop(0)()
            grad.take_far(stage - 1)
    grad.take_halo(True)
    backward.add(0)
    while len(later) > 1:
        later.pop(0)()
    grad.take_halo(False)
    backward.add(size_x + 1)
    later.pop(0)()
    grad.take_far(stages - 1)
    backward.add(done[-1])
    reduce.last()
    weight_ref[...] = result[0 : weight_ref.shape[0]].astype(F32)
    vol.finish()
    grad.finish()
    weights.finish()
    reduce.finish()


def on_device(volume, kernel, bias, cotangent):
    size_x, size_y, part, size_z = volume.shape
    taps, outs, chans = kernel.shape
    shape = jax.ShapeDtypeStruct
    flops = 2 * size_x * size_y * size_z * taps * outs * chans
    peers, slabs = lax.axis_size("chan"), lax.axis_size("space")
    each = max(1, size_z // part)
    groups = 2 * -(-taps // (2 * each))
    members = slabs // 2
    chunk = 16 * -(-taps * outs // (slabs * 16))
    whole = pl.BlockSpec(memory_space=pltpu.VMEM)
    args = (volume, kernel.reshape(3, 3, 3 * outs, chans), bias.reshape(1, outs), cotangent)
    planes = size_x + 2
    dma = pltpu.SemaphoreType.DMA
    sides = [dma((planes, peers, 2)), dma((planes, peers, 2)), dma((2, peers)), dma((2, peers))]
    output, input_grad, weight_grad = pl.pallas_call(
        functools.partial(fused_kernel, peers, slabs),
        out_shape=(
            shape(cotangent.shape, BF16),
            shape(volume.shape, BF16),
            shape((taps * outs, chans), F32),
        ),
        in_specs=[pl.BlockSpec(memory_space=pl.ANY)] + [whole] * 3,
        out_specs=(whole, whole, whole),
        scratch_shapes=[
            pltpu.VMEM((planes * chans, (size_y + 2) * size_z), BF16),
            pltpu.VMEM((planes * chans, (size_y + 2) * size_z), BF16),
            pltpu.VMEM((size_x, 3 * outs, size_y * size_z), F32),
            pltpu.VMEM((size_x, 3 * outs, size_y * size_z), BF16),
            pltpu.VMEM((slabs * chunk, chans), F32),
            pltpu.VMEM((members * chunk, chans), BF16),
            pltpu.VMEM((members * chunk, chans), BF16),
            pltpu.VMEM((members * chunk, chans), BF16),
            pltpu.VMEM((members, chunk, chans), BF16),
            pltpu.VMEM((slabs * chunk, chans), BF16),
            pltpu.VMEM((peers, groups, outs, each * part), BF16),
            pltpu.VMEM((peers, groups, outs, each * part), BF16),
            pltpu.VMEM((3, 3, 3 * part, chans), BF16),
            dma((planes,)),
            *sides,
            *sides,
            dma(()),
            dma((peers,)),
            dma((peers,)),
            dma((peers,)),
            dma((peers,)),
            dma(()),
            dma(()),
            *[dma((members,)) for _ in range(6)],
        ],
        compiler_params=pltpu.CompilerParams(vmem_limit_bytes=VMEM_LIMIT, collective_id=0, has_side_effects=True),
        cost_estimate=pl.CostEstimate(flops=3 * flops, bytes_accessed=8 * volume.size, transcendentals=0),
    )(*args)
    return output, input_grad, weight_grad.reshape(taps, outs, chans)


def solution(mesh):
    return jax.shard_map(
        on_device,
        mesh=mesh,
        in_specs=(
            P("space", None, "chan", None),
            P(None, "chan", None),
            P("chan"),
            P("space", None, "chan", None),
        ),
        out_specs=(
            P("space", None, "chan", None),
            P("space", None, "chan", None),
            P(None, "chan", None),
        ),
        check_vma=False,
    )
```
